256 devices in a mesh: rows: 64 (over z, y, core), grp: 4 (over x).
Axes of the slice: x: 4, y: 4, z: 8, core: 2. Of those that a mesh axis runs over, the one named last changes fastest.
Arguments:
- matrix: float32 [524288, 512], P(('rows', 'grp')), may hold values from -6 to 6
- sign_bits: int32 [524288], P(('rows', 'grp')), may hold values from 0 to 1
- samples: int32 [16, 16384], P('grp'), may hold values from 0 to 32767, as said below
Outputs:
- r_factor: float32 [512, 512], replicated
- solved: float32 [524288, 512], P(('rows', 'grp'))
The draws below stay inside these ranges and needn't reach their ends.
Inputs may be any that keep to these rules, and one draw needn't show every extreme that they name: `samples`: each row names 16384 distinct positions of a batch, exactly one of each pair 2 k and 2 k + 1, in any order.
All inputs are finite; a program needn't handle non-finite values.
Results may differ from the reference program's by a relative error of at most 0.0001.
Values sent between devices are 32-bit elements; how exact they have to be, the bound alone decides.
No kernel may reach another device: no remote copies, remote signals or barrier semaphores. Data moves between devices by JAX's collectives and lax.ppermute only.
A program may use at most 128 MiB of HBM per device.

```python
import jax
import jax.numpy as jnp
from jax import lax

COLS = 512
LENGTH = 32768
INNER = 256
BATCHES = 4
PER_DEV = 512
HALF = 16384
M = 524288
N_ROWS = 64
N_GRP = 4


def draw_samples(key, part):

    def single(subkey):
        first, second = jax.random.split(subkey)
        pairs = jax.random.permutation(first, HALF).astype(jnp.int32)
        chosen = jax.random.randint(second, (HALF,), 0, 2).astype(jnp.int32)
        chosen = jnp.where(pairs == 0, 0, jnp.where(pairs == HALF - 1, 1, chosen))
        return (2 * pairs + chosen).astype(jnp.int32)
    subkeys = jax.random.split(jax.random.fold_in(key, 17), N_GRP * BATCHES)
    return jax.vmap(single)(subkeys)


def with_ends(result, own_key, smallest, largest):
    longest = result.shape.index(max(result.shape))
    spots = []
    for shift in (0, 1):
        where = [jax.random.randint(jax.random.fold_in(own_key, axis), (), 0, length) for axis, length in enumerate(result.shape)]
        where[longest] = (where[longest] + shift) % result.shape[longest]
        spots.append(tuple(where))
    return result.at[spots[0]].set(smallest).at[spots[1]].set(largest)


def levels(stream_key, shape, cuts, smallest, top_value):
    level = 1.0
    for position, shards_of in cuts:
        heights = jax.random.uniform(jax.random.fold_in(jax.random.fold_in(stream_key, 6), position), (shards_of,), jnp.float32, smallest / len(cuts), top_value / len(cuts))
        level = level * jnp.repeat(jnp.exp(heights), shape[position] // shards_of).reshape((-1,) + (1,) * (len(shape) - 1 - position))
    return level


def bell_draw(own_key, shape, deviation, limit, pieces=(), kind=jnp.bfloat16):
    entries = jax.random.normal(own_key, shape, jnp.float32) * deviation
    if len(pieces) > 0:
        entries = levels(own_key, shape, pieces, -0.22, 0.18) * entries
    return jnp.clip(entries, min=-limit, max=limit).astype(kind)


def setup_inputs(seed: int = 0) -> dict:
    key_list = jax.random.split(jax.random.key(seed), 4)
    matrix = bell_draw(key_list[0], (M, COLS), 1.0, 6.0, ((0, 256),), jnp.float32)
    sign_bits = with_ends(jax.random.randint(key_list[1], (M,), 0, 2), jax.random.fold_in(key_list[1], 1), 0, 1).astype(jnp.int32)
    samples = draw_samples(jax.random.fold_in(key_list[3], 71), 0)
    return {"matrix": matrix, "sign_bits": sign_bits, "samples": samples}


def cosine(size):
    freq = jnp.arange(size, dtype=jnp.int32)[:, None]
    place = jnp.arange(size, dtype=jnp.int32)[None, :]
    phase = (2 * place + 1) * freq % (4 * size)
    weight = jnp.where(freq == 0, 1.0, 2.0).astype(jnp.float32) / size
    return jnp.sqrt(weight) * jnp.cos(jnp.pi * phase.astype(jnp.float32) / (2 * size))

def reference(matrix, sign_bits, samples):
    signed = matrix * (1 - 2 * sign_bits).astype(jnp.float32)[:, None]
    blocks = signed.reshape(N_ROWS, N_GRP, BATCHES, PER_DEV, COLS)
    c_outer = cosine(LENGTH // INNER)
    c_inner = cosine(INNER)
    gram = jnp.zeros((COLS, COLS), jnp.float32)
    for group in range(N_GRP):
        for batch in range(BATCHES):
            stacked = blocks[:, group, batch].reshape(LENGTH // INNER, INNER, COLS)
            mixed = jnp.einsum('ap,pqn->aqn', c_outer, stacked, precision=lax.Precision.HIGHEST)
            mixed = jnp.einsum('bq,aqn->abn', c_inner, mixed, precision=lax.Precision.HIGHEST)
            mixed = mixed.reshape(LENGTH, COLS)
            picked = mixed[samples[group * BATCHES + batch]]
            gram = gram + jnp.dot(picked.T.astype(jnp.float32), picked.astype(jnp.float32), precision=lax.Precision.HIGHEST, preferred_element_type=jnp.float32)
    gram = gram / (N_GRP * BATCHES * HALF)
    lower = jnp.linalg.cholesky(gram)
    inverse = jax.scipy.linalg.solve_triangular(lower, jnp.eye(COLS, dtype=jnp.float32), lower=True)
    solved = jnp.dot(matrix.astype(jnp.float32), inverse.T.astype(jnp.float32), precision=lax.Precision.HIGHEST, preferred_element_type=jnp.float32)
    return (lower.T, solved)
```

```python
import functools
import numpy as np
import jax
import jax.numpy as jnp
from jax import lax
from jax.sharding import Mesh
from jax.sharding import PartitionSpec as P
from jax.experimental import pallas as pl
from jax.experimental.pallas import tpu as pltpu

F32, BF16 = jnp.float32, jnp.bfloat16
NT = (((1,), (1,)), ((), ()))
TN = (((0,), (0,)), ((), ()))


def cosine64(size):
    freq = np.arange(size)[:, None]
    place = np.arange(size)[None, :]
    weight = np.where(freq == 0, 1.0, 2.0) / size
    return np.sqrt(weight) * np.cos(np.pi * ((2 * place + 1) * freq % (4 * size)) / (2 * size))


def two(table):
    high = table.astype(np.float32).astype(jnp.bfloat16)
    low = (table - high.astype(np.float64)).astype(np.float32).astype(jnp.bfloat16)
    return high, low


def inner_tables():
    table = cosine64(256)
    swapped = table.reshape(32, 2, 4, 256)[:, ::-1].reshape(256, 256)
    return two(np.stack([table, swapped]))


def outer_tables():
    table = cosine64(128).reshape(128, 64, 2)
    both = np.stack([table, table[:, :, ::-1]])
    wide = np.broadcast_to(both[:, None, :, :, :, None], (2, 2, 128, 64, 2, 4))
    return two(wide.reshape(2, 256, 512))


def split(x):
    high = x.astype(BF16)
    return high, (x - high.astype(F32)).astype(BF16)


def dot(a, b, dims=(((1,), (0,)), ((), ()))):
    return lax.dot_general(a, b, dims, preferred_element_type=F32)


def inner_kernel(sign_ref, high_ref, low_ref, x_ref, out_ref):
    results = []
    for s in range(2):
        place = 4 * pl.program_id(0) + 2 * s
        bits = jnp.concatenate([sign_ref[pl.ds(place, 1), :], sign_ref[pl.ds(place + 1, 1), :]], axis=1)
        sign = (1 - 2 * bits).astype(F32).astype(BF16)
        ch, cl = high_ref[s] * sign, low_ref[s] * sign
        xh, xl = split(x_ref[s * 256 : (s + 1) * 256, :])
        results.append((dot(ch, xh) + (dot(cl, xh) + dot(ch, xl))).reshape(32, 8, 512))
    first, second = results
    upper = lax.broadcasted_iota(jnp.int32, first.shape, 1) < 4
    out_ref[:, 0, 0] = jnp.where(upper, first, second)
    out_ref[:, 1, 0] = jnp.where(upper, second, first)


def inner(matrix, sign_bits):
    batches = matrix.shape[0] // 512
    high, low = inner_tables()
    whole = pl.BlockSpec((2, 256, 256), lambda b: (0, 0, 0))
    return pl.pallas_call(
        inner_kernel,
        grid=(batches,),
        in_specs=[
            pl.BlockSpec((4 * batches, 128), lambda b: (0, 0)),
            whole,
            whole,
            pl.BlockSpec((512, 512), lambda b: (b, 0)),
        ],
        out_specs=pl.BlockSpec((32, 2, 1, 8, 512), lambda b: (0, 0, b, 0, 0)),
        out_shape=jax.ShapeDtypeStruct((32, 2, batches, 8, 512), F32),
        name="inner",
    )(sign_bits.reshape(4 * batches, 128), jnp.asarray(high), jnp.asarray(low), matrix)


def parity_kernel(first_ref, samples_ref, out_ref):
    batches, half = samples_ref.shape[0], samples_ref.shape[1]
    first = first_ref[0]
    step = 2048
    for b in range(batches):
        total = jnp.zeros((8, 128), F32)
        for start in range(0, half, step):
            pos = samples_ref[b : b + 1, start : start + step]
            a = lax.shift_right_logical(pos, 8)
            pair = lax.shift_right_logical(lax.bitwise_and(pos, 255), 1) - first
            odd = lax.bitwise_and(pos, 1)
            rows = lax.broadcasted_iota(jnp.int32, (128, step), 0)
            hot = (rows == a).astype(F32).astype(BF16)
            which = lax.broadcasted_iota(jnp.int32, (8, step), 0)
            mine = jnp.where(which == pair, odd, 0).astype(F32).astype(BF16)
            total = total + dot(mine, hot, NT)
        out_ref[b] = total


def parity(samples, first_pair):
    batches, half = samples.shape
    return pl.pallas_call(
        parity_kernel,
        grid_spec=pltpu.PrefetchScalarGridSpec(
            num_scalar_prefetch=1,
            grid=(1,),
            in_specs=[pl.BlockSpec((batches, half), lambda i, f: (0, 0))],
            out_specs=pl.BlockSpec((batches, 8, 128), lambda i, f: (0, 0, 0)),
        ),
        out_shape=jax.ShapeDtypeStruct((batches, 8, 128), F32),
        cost_estimate=pl.CostEstimate(flops=2 * batches * half * 128 * 8, bytes_accessed=4 * batches * half, transcendentals=0),
        name="parity",
    )(first_pair, samples)


def outer_kernel(scale, steps, par_ref, odd_ref, high_ref, low_ref, z_ref, keep_ref, send_ref, acc_ref):
    step = pl.program_id(0)
    z = z_ref[:, 0].reshape(512, 512)
    zh, zl = split(z)
    row = lax.broadcasted_iota(jnp.int32, (256, 512), 0)
    col = lax.broadcasted_iota(jnp.int32, (256, 512), 1)
    choice = 2 * lax.shift_right_logical(row, 7) + odd_ref[0].astype(jnp.int32)
    keep = jnp.where(lax.bitwise_and(col, 3) == choice, 1.0, 0.0).astype(BF16)
    wh, wl = high_ref[0] * keep, low_ref[0] * keep
    rows = dot(wh, zh) + (dot(wl, zh) + dot(wh, zl))
    rh, rl = split(rows)
    part = dot(rh, rh, TN) + (dot(rh, rl, TN) + dot(rl, rh, TN))

    @pl.when(step == 0)
    def _():
        acc_ref[...] = part

    @pl.when(step > 0)
    def _():
        acc_ref[...] += part

    @pl.when(step == steps - 1)
    def _():
        mine = pl.multiple_of(256 * par_ref[0], 256)
        keep_ref[...] = acc_ref[pl.ds(mine, 256), :] * scale
        send_ref[...] = acc_ref[pl.ds(256 - mine, 256), :] * scale


def outer(mixed, odd, par, scale):
    batches = mixed.shape[1]
    high, low = outer_tables()
    table = pl.BlockSpec((1, 256, 512), lambda b, p: (p[0], 0, 0))
    return pl.pallas_call(
        functools.partial(outer_kernel, scale, batches),
        grid_spec=pltpu.PrefetchScalarGridSpec(
            num_scalar_prefetch=1,
            grid=(batches,),
            in_specs=[
                pl.BlockSpec((1, 256, 1), lambda b, p: (b, 0, 0)),
                table,
                table,
                pl.BlockSpec((64, 1, 8, 512), lambda b, p: (0, b, 0, 0)),
            ],
            out_specs=[pl.BlockSpec((256, 512), lambda b, p: (0, 0))] * 2,
            scratch_shapes=[pltpu.VMEM((512, 512), F32)],
        ),
        out_shape=[jax.ShapeDtypeStruct((256, 512), F32)] * 2,
        name="outer",
    )(par, odd, jnp.asarray(high), jnp.asarray(low), mixed)


def hdot(a, b, dims=(((1,), (0,)), ((), ()))):
    return lax.dot_general(a, b, dims, precision=lax.Precision.HIGHEST, preferred_element_type=F32)


def factor(block):
    size = block.shape[0]
    lane = lax.broadcasted_iota(jnp.int32, (1, size), 1)
    groups = [block[8 * i : 8 * i + 8] for i in range(size // 8)]
    sub = lax.broadcasted_iota(jnp.int32, (8, size), 0)
    pivots = jnp.zeros((1, size), F32)
    pivot_rows = []
    for j in range(size):
        g, r = j // 8, j % 8
        row = groups[g][r : r + 1]
        pivot = row[:, j : j + 1]
        inverse = 1.0 / pivot
        row = jnp.where(lane == j, 1.0, row) * inverse
        pivot_rows.append(pivot)
        for i in range(g, size // 8):
            if i == g and r == 7:
                continue
            column = groups[i][:, j : j + 1]
            if i == g:
                column = jnp.where(sub[:, :1] > r, column, 0.0)
                rest = jnp.where((lane == j) & (sub > r), 0.0, groups[i])
            else:
                rest = jnp.where(lane == j, 0.0, groups[i])
            groups[i] = rest - column * row
    return jnp.concatenate(groups, axis=0), jnp.concatenate(pivot_rows, axis=0)


def solve_kernel(par_ref, own_ref, other_ref, x_ref, r_ref, out_ref, g_ref, inv_ref, xh_ref, xl_ref):
    n, nb = 512, 128
    mine = pl.multiple_of(256 * par_ref[0], 256)
    g_ref[pl.ds(mine, 256), :] = own_ref[...]
    g_ref[pl.ds(256 - mine, 256), :] = other_ref[...]
    inv_ref[...] = jnp.zeros((n, n), F32)
    r_ref[...] = jnp.zeros((n, n), F32)
    xh, xl = split(x_ref[...])
    xh_ref[...] = xh
    xl_ref[...] = xl
    row = lax.broadcasted_iota(jnp.int32, (nb, nb), 0)
    col = lax.broadcasted_iota(jnp.int32, (nb, nb), 1)
    for k in range(n // nb):
        lo, hi = k * nb, (k + 1) * nb
        m, pivots = factor(g_ref[lo:hi, lo:hi])
        root = lax.rsqrt(pivots)
        root = root * (1.5 - 0.5 * pivots * root * root)
        upper = jnp.where(col > row, m, jnp.where(col == row, pivots, 0.0)) * root
        linv = jnp.where(col < row, m, jnp.where(col == row, 1.0, 0.0)) * root
        r_ref[lo:hi, lo:hi] = upper
        rinv = linv.T
        inv_ref[lo:hi, lo:hi] = rinv
        if k + 1 < n // nb:
            panel = hdot(linv, g_ref[lo:hi, hi:])
            r_ref[lo:hi, hi:] = panel
            g_ref[hi:, hi:] -= hdot(panel, panel, TN)
        if k > 0:
            t = hdot(inv_ref[:lo, :lo], r_ref[:lo, lo:hi])
            inv_ref[:lo, lo:hi] = -hdot(t, rinv)
        ih, il = split(inv_ref[:hi, lo:hi])
        a, b = xh_ref[:, :hi], xl_ref[:, :hi]
        out_ref[:, lo:hi] = dot(a, ih) + (dot(b, ih) + dot(a, il))


def solve(par, own, other, matrix):
    rows, n = matrix.shape
    vmem = pl.BlockSpec(memory_space=pltpu.VMEM)
    smem = pl.BlockSpec(memory_space=pltpu.SMEM)
    return pl.pallas_call(
        solve_kernel,
        in_specs=[smem, vmem, vmem, vmem],
        out_specs=(vmem, vmem),
        out_shape=(jax.ShapeDtypeStruct((n, n), F32), jax.ShapeDtypeStruct((rows, n), F32)),
        scratch_shapes=[
            pltpu.VMEM((n, n), F32),
            pltpu.VMEM((n, n), F32),
            pltpu.VMEM((rows, n), BF16),
            pltpu.VMEM((rows, n), BF16),
        ],
        compiler_params=pltpu.CompilerParams(vmem_limit_bytes=48 * 2**20),
        name="solve",
    )(par, own, other, matrix)


def exchange(x, axes):
    return lax.all_to_all(x, axes, split_axis=0, concat_axis=0, tiled=True)


def spread(x, copies, axes):
    return exchange(jnp.broadcast_to(x[None], (copies,) + x.shape), axes)


def local(matrix, sign_bits, samples):
    batches, half = samples.shape
    core = lax.axis_index("core").astype(jnp.int32)
    device = lax.axis_index(("z", "y", "core")).astype(jnp.int32)
    par = core.reshape(1)
    sent = inner(matrix, sign_bits).reshape(64, batches, 8, 512)
    mixed = exchange(sent, ("z", "y", "core"))
    odd = parity(samples, (2 * device).reshape(1))[:, :2].reshape(batches, 256, 1)
    keep, send = outer(mixed, odd, par, 1.0 / (4 * batches * half))
    swap = [(0, 1), (1, 0)]
    part = keep + lax.ppermute(send, "core", swap)
    part = exchange(part.reshape(16, 16, 512), ("y", "x")).sum(0)
    part = spread(part, 8, "z").sum(0)
    own = spread(part, 16, ("y", "x")).reshape(256, 512)
    other = lax.ppermute(own, "core", swap)
    return solve(par, own, other, matrix)


def solution(mesh):
    parts = Mesh(mesh.devices.reshape(8, 4, 2, 4), ("z", "y", "core", "x"))
    every = ("z", "y", "core", "x")
    return jax.shard_map(
        local,
        mesh=parts,
        in_specs=(P(every, None), P(every), P("x", None)),
        out_specs=(P(), P(every, None)),
        check_vma=False,
    )
```

```python
import functools
import numpy as np
import jax
import jax.numpy as jnp
from jax import lax
from jax.sharding import Mesh
from jax.sharding import PartitionSpec as P
from jax.experimental import pallas as pl
from jax.experimental.pallas import tpu as pltpu

F32, BF16 = jnp.float32, jnp.bfloat16
NT = (((1,), (1,)), ((), ()))
TN = (((0,), (0,)), ((), ()))


def cosine64(size):
    freq = np.arange(size)[:, None]
    place = np.arange(size)[None, :]
    weight = np.where(freq == 0, 1.0, 2.0) / size
    return np.sqrt(weight) * np.cos(np.pi * ((2 * place + 1) * freq % (4 * size)) / (2 * size))


def two(table):
    high = table.astype(np.float32).astype(jnp.bfloat16)
    low = (table - high.astype(np.float64)).astype(np.float32).astype(jnp.bfloat16)
    return high, low


def inner_tables():
    table = cosine64(256)
    swapped = table.reshape(32, 2, 4, 256)[:, ::-1].reshape(256, 256)
    return two(np.stack([table, swapped]))


def split(x):
    high = x.astype(BF16)
    return high, (x - high.astype(F32)).astype(BF16)


def dot(a, b, dims=(((1,), (0,)), ((), ()))):
    return lax.dot_general(a, b, dims, preferred_element_type=F32)


def inner_kernel(start, sign_ref, high_ref, low_ref, x_ref, out_ref):
    results = []
    for s in range(2):
        place = 4 * (start + pl.program_id(0)) + 2 * s
        bits = jnp.concatenate([sign_ref[pl.ds(place, 1), :], sign_ref[pl.ds(place + 1, 1), :]], axis=1)
        sign = (1 - 2 * bits).astype(F32).astype(BF16)
        ch, cl = high_ref[s] * sign, low_ref[s] * sign
        xh, xl = split(x_ref[s * 256 : (s + 1) * 256, :])
        results.append((dot(ch, xh) + (dot(cl, xh) + dot(ch, xl))).reshape(32, 8, 512))
    first, second = results
    upper = lax.broadcasted_iota(jnp.int32, first.shape, 1) < 4
    out_ref[:, 0, 0] = jnp.where(upper, first, second)
    out_ref[:, 1, 0] = jnp.where(upper, second, first)


def inner(matrix, sign_bits, start, count):
    high, low = inner_tables()
    whole = pl.BlockSpec((2, 256, 256), lambda b: (0, 0, 0))
    return pl.pallas_call(
        functools.partial(inner_kernel, start),
        grid=(count,),
        in_specs=[
            pl.BlockSpec((matrix.shape[0] // 128, 128), lambda b: (0, 0)),
            whole,
            whole,
            pl.BlockSpec((512, 512), lambda b: (start + b, 0)),
        ],
        out_specs=pl.BlockSpec((32, 2, 1, 8, 512), lambda b: (0, 0, b, 0, 0)),
        out_shape=jax.ShapeDtypeStruct((32, 2, count, 8, 512), F32),
        cost_estimate=pl.CostEstimate(flops=count * 6 * 512 * 256 * 512, bytes_accessed=count * 2**21, transcendentals=0),
        name="inner",
    )(sign_bits.reshape(-1, 128), jnp.asarray(high), jnp.asarray(low), matrix)


def parity_kernel(first_ref, samples_ref, out_ref):
    batches, half = samples_ref.shape[0], samples_ref.shape[1]
    first = first_ref[0]
    step = 2048
    for b in range(batches):
        total = jnp.zeros((8, 128), F32)
        for start in range(0, half, step):
            pos = samples_ref[b : b + 1, start : start + step]
            a = lax.shift_right_logical(pos, 8)
            pair = lax.shift_right_logical(lax.bitwise_and(pos, 255), 1) - first
            odd = lax.bitwise_and(pos, 1)
            rows = lax.broadcasted_iota(jnp.int32, (128, step), 0)
            hot = (rows == a).astype(F32).astype(BF16)
            which = lax.broadcasted_iota(jnp.int32, (8, step), 0)
            mine = jnp.where(which == pair, odd, 0).astype(F32).astype(BF16)
            total = total + dot(mine, hot, NT)
        out_ref[b] = total


def parity(samples, first_pair):
    batches, half = samples.shape
    return pl.pallas_call(
        parity_kernel,
        grid_spec=pltpu.PrefetchScalarGridSpec(
            num_scalar_prefetch=1,
            grid=(1,),
            in_specs=[pl.BlockSpec((batches, half), lambda i, f: (0, 0))],
            out_specs=pl.BlockSpec((batches, 8, 128), lambda i, f: (0, 0, 0)),
        ),
        out_shape=jax.ShapeDtypeStruct((batches, 8, 128), F32),
        cost_estimate=pl.CostEstimate(flops=2 * batches * half * 128 * 8, bytes_accessed=4 * batches * half, transcendentals=0),
        name="parity",
    )(first_pair, samples)


def outer_kernel(scale, steps, par_ref, odd_ref, high_ref, low_ref, z_ref, prev_ref, *refs):
    step = pl.program_id(0)
    acc_ref, wide_ref = refs[-2:]

    @pl.when(step == 0)
    def _():
        acc_ref[...] = jnp.zeros((512, 512), F32) if prev_ref is None else prev_ref[...]
        place = lax.broadcasted_iota(jnp.int32, (128, 512), 0)
        col = lax.broadcasted_iota(jnp.int32, (128, 512), 1)
        source = 2 * lax.shift_right_logical(col, 3) + lax.bitwise_xor(
            lax.bitwise_and(lax.shift_right_logical(col, 2), 1), par_ref[0]
        )
        pick = jnp.where(place == source, 1.0, 0.0).astype(BF16)
        wide_ref[0] = dot(high_ref[...], pick).astype(BF16)
        wide_ref[1] = dot(low_ref[...], pick).astype(BF16)

    z = z_ref[:, 0].reshape(512, 512)
    zh, zl = split(z)
    row = lax.broadcasted_iota(jnp.int32, (256, 512), 0)
    col = lax.broadcasted_iota(jnp.int32, (256, 512), 1)
    choice = 2 * lax.shift_right_logical(row, 7) + odd_ref[0].astype(jnp.int32)
    keep = jnp.where(lax.bitwise_and(col, 3) == choice, 1.0, 0.0).astype(BF16)
    wh = jnp.concatenate([wide_ref[0]] * 2, axis=0) * keep
    wl = jnp.concatenate([wide_ref[1]] * 2, axis=0) * keep
    rows = dot(wh, zh) + (dot(wl, zh) + dot(wh, zl))
    rh, rl = split(rows)
    acc_ref[...] += dot(rh, rh, TN) + (dot(rh, rl, TN) + dot(rl, rh, TN))

    @pl.when(step == steps - 1)
    def _():
        if scale is None:
            refs[0][...] = acc_ref[...]
        else:
            mine = pl.multiple_of(256 * par_ref[0], 256)
            refs[0][...] = acc_ref[pl.ds(mine, 256), :] * scale
            refs[1][...] = acc_ref[pl.ds(256 - mine, 256), :] * scale


def outer(mixed, odd, start, par, prev, scale):
    count = mixed.shape[1]
    high, low = two(cosine64(128))
    table = pl.BlockSpec((128, 128), lambda b, p: (0, 0))
    whole = pl.BlockSpec((512, 512), lambda b, p: (0, 0))
    half = pl.BlockSpec((256, 512), lambda b, p: (0, 0))
    body = functools.partial(outer_kernel, scale, count)
    if prev is None:
        kernel = lambda p, o, h, l, z, *refs: body(p, o, h, l, z, None, *refs)
    else:
        kernel = body
    return pl.pallas_call(
        kernel,
        grid_spec=pltpu.PrefetchScalarGridSpec(
            num_scalar_prefetch=1,
            grid=(count,),
            in_specs=[
                pl.BlockSpec((1, 256, 1), lambda b, p: (start + b, 0, 0)),
                table,
                table,
                pl.BlockSpec((64, 1, 8, 512), lambda b, p: (0, b, 0, 0)),
            ]
            + ([] if prev is None else [whole]),
            out_specs=whole if scale is None else [half, half],
            scratch_shapes=[pltpu.VMEM((512, 512), F32), pltpu.VMEM((2, 128, 512), BF16)],
        ),
        out_shape=jax.ShapeDtypeStruct((512, 512), F32)
        if scale is None
        else [jax.ShapeDtypeStruct((256, 512), F32)] * 2,
        cost_estimate=pl.CostEstimate(flops=count * 12 * 256 * 512 * 512, bytes_accessed=count * 2**20, transcendentals=0),
        name="outer",
    )(par, odd, jnp.asarray(high), jnp.asarray(low), mixed, *([] if prev is None else [prev]))


def hdot(a, b, dims=(((1,), (0,)), ((), ()))):
    return lax.dot_general(a, b, dims, precision=lax.Precision.HIGHEST, preferred_element_type=F32)


def factor(block):
    size = block.shape[0]
    lane = lax.broadcasted_iota(jnp.int32, (8, size), 1)
    sub = lax.broadcasted_iota(jnp.int32, (8, size), 0)
    count = size // 8
    rows = [block[8 * i : 8 * i + 8] for i in range(count)]
    pivots = []

    def along(x, c):
        return jnp.broadcast_to(x[:, c : c + 1], (8, size))

    def down(x, j):
        return jnp.broadcast_to(x[j : j + 1, :], (8, size))

    for r in range(count):
        first = 8 * r
        inside = (lane >= first) & (lane < first + 8)
        below = range(r + 1, count)
        cols = {i: [along(rows[i], first + k) for k in range(8)] for i in range(r, count)}
        own = jnp.where(inside, jnp.where(lane - first == sub, 1.0, 0.0), rows[r])
        rest = {i: jnp.where(inside, 0.0, rows[i]) for i in below}
        for j in range(8):
            inverse = 1.0 / down(cols[r][j], j)
            heads = {k: down(cols[r][k], j) for k in range(j + 1, 8)}
            line = down(own, j)
            for i in range(r, count):
                factor = cols[i][j] * inverse
                if i == r:
                    if j == 7:
                        continue
                    factor = jnp.where(sub > j, factor, 0.0)
                for k in range(j + 1, 8):
                    cols[i][k] = cols[i][k] - factor * heads[k]
                if i == r:
                    own = own - factor * line
                else:
                    rest[i] = rest[i] - factor * line
        pivot = cols[r][0]
        for k in range(8):
            own = jnp.where((lane == first + k) & (sub <= k), cols[r][k], own)
            if k > 0:
                pivot = jnp.where(sub == k, cols[r][k], pivot)
        rows[r] = own
        pivots.append(pivot)
        for i in below:
            rows[i] = rest[i]
    return jnp.concatenate(rows, axis=0), jnp.concatenate(pivots, axis=0)


def solve_kernel(par_ref, own_ref, other_ref, x_hbm, r_ref, out_hbm, g_ref, inv_ref, x_ref, xh_ref, xl_ref, out_ref, in_sem, out_sem):
    n, nb = 512, 128
    count = n // nb
    fetch = pltpu.make_async_copy(x_hbm, x_ref, in_sem)
    fetch.start()
    mine = pl.multiple_of(256 * par_ref[0], 256)
    g_ref[pl.ds(mine, 256), :] = own_ref[...]
    g_ref[pl.ds(256 - mine, 256), :] = other_ref[...]
    inv_ref[...] = jnp.zeros((n, n), F32)
    r_ref[...] = jnp.zeros((n, n), F32)
    row = lax.broadcasted_iota(jnp.int32, (nb, nb), 0)
    col = lax.broadcasted_iota(jnp.int32, (nb, nb), 1)
    stores = []
    for k in range(count):
        lo, hi = k * nb, (k + 1) * nb
        m, pivots = factor(g_ref[lo:hi, lo:hi])
        root = lax.rsqrt(pivots)
        root = root * (1.5 - 0.5 * pivots * root * root)
        upper = jnp.where(col >= row, m, 0.0) * root
        linv = jnp.where(col < row, m, jnp.where(col == row, 1.0, 0.0)) * root
        r_ref[lo:hi, lo:hi] = upper
        panels = {}
        for j in range(k + 1, count):
            a, b = j * nb, (j + 1) * nb
            panels[j] = hdot(linv, g_ref[lo:hi, a:b])
            r_ref[lo:hi, a:b] = panels[j]
            for i in range(k + 1, j + 1):
                c, d = i * nb, (i + 1) * nb
                g_ref[c:d, a:b] -= hdot(panels[i], panels[j], TN)
        rinv = linv.T
        inv_ref[lo:hi, lo:hi] = rinv
        if k > 0:
            t = hdot(inv_ref[:lo, :lo], r_ref[:lo, lo:hi])
            inv_ref[:lo, lo:hi] = -hdot(t, rinv)
        if k == 0:
            fetch.wait()
            xh, xl = split(x_ref[...])
            xh_ref[...] = xh
            xl_ref[...] = xl
        ih, il = split(inv_ref[:hi, lo:hi])
        a, b = xh_ref[:, :hi], xl_ref[:, :hi]
        out_ref[k] = dot(a, ih) + (dot(b, ih) + dot(a, il))
        store = pltpu.make_async_copy(out_ref.at[k], out_hbm.at[:, lo:hi], out_sem.at[k])
        store.start()
        stores.append(store)
    for store in stores:
        store.wait()


def solve(par, own, other, matrix):
    rows, n = matrix.shape
    vmem = pl.BlockSpec(memory_space=pltpu.VMEM)
    smem = pl.BlockSpec(memory_space=pltpu.SMEM)
    hbm = pl.BlockSpec(memory_space=pltpu.HBM)
    return pl.pallas_call(
        solve_kernel,
        in_specs=[smem, vmem, vmem, hbm],
        out_specs=(vmem, hbm),
        out_shape=(jax.ShapeDtypeStruct((n, n), F32), jax.ShapeDtypeStruct((rows, n), F32)),
        scratch_shapes=[
            pltpu.VMEM((n, n), F32),
            pltpu.VMEM((n, n), F32),
            pltpu.VMEM((rows, n), F32),
            pltpu.VMEM((rows, n), BF16),
            pltpu.VMEM((rows, n), BF16),
            pltpu.VMEM((n // 128, rows, 128), F32),
            pltpu.SemaphoreType.DMA,
            pltpu.SemaphoreType.DMA((n // 128,)),
        ],
        compiler_params=pltpu.CompilerParams(vmem_limit_bytes=61 * 2**20),
        name="solve",
    )(par, own, other, matrix)


def exchange(x, axes):
    return lax.all_to_all(x, axes, split_axis=0, concat_axis=0, tiled=True)


def spread(x, copies, axes):
    return exchange(jnp.broadcast_to(x[None], (copies,) + x.shape), axes)


def local(matrix, sign_bits, samples):
    batches, half = samples.shape
    core = lax.axis_index("core").astype(jnp.int32)
    device = lax.axis_index(("z", "y", "core")).astype(jnp.int32)
    par = core.reshape(1)
    mixed = []
    start = 0
    for count in (batches,):
        sent = inner(matrix, sign_bits, start, count).reshape(64, count, 8, 512)
        mixed.append(exchange(sent, ("z", "y", "core")))
        start += count
    odd = parity(samples, (2 * device).reshape(1))[:, :2].reshape(batches, 256, 1)
    start, total = 0, None
    for i, count in enumerate((batches,)):
        last = i == len(mixed) - 1
        total = outer(mixed[i], odd, start, par, total, 1.0 / (4 * batches * half) if last else None)
        start += count
    keep, send = total
    swap = [(0, 1), (1, 0)]
    part = keep + lax.ppermute(send, "core", swap)
    part = exchange(part.reshape(16, 16, 512), ("y", "x")).sum(0)
    part = spread(part, 8, "z").sum(0)
    own = spread(part, 16, ("y", "x")).reshape(256, 512)
    other = lax.ppermute(own, "core", swap)
    return solve(par, own, other, matrix)


def solution(mesh):
    parts = Mesh(mesh.devices.reshape(8, 4, 2, 4), ("z", "y", "core", "x"))
    every = ("z", "y", "core", "x")
    return jax.shard_map(
        local,
        mesh=parts,
        in_specs=(P(every, None), P(every), P("x", None)),
        out_specs=(P(), P(every, None)),
        check_vma=False,
    )
```

```python
import functools
import numpy as np
import jax
import jax.numpy as jnp
from jax import lax
from jax.sharding import Mesh
from jax.sharding import PartitionSpec as P
from jax.experimental import pallas as pl
from jax.experimental.pallas import tpu as pltpu

F32, BF16 = jnp.float32, jnp.bfloat16
NT = (((1,), (1,)), ((), ()))
TN = (((0,), (0,)), ((), ()))


def cosine64(size):
    freq = np.arange(size)[:, None]
    place = np.arange(size)[None, :]
    weight = np.where(freq == 0, 1.0, 2.0) / size
    return np.sqrt(weight) * np.cos(np.pi * ((2 * place + 1) * freq % (4 * size)) / (2 * size))


def two(table):
    high = table.astype(np.float32).astype(jnp.bfloat16)
    low = (table - high.astype(np.float64)).astype(np.float32).astype(jnp.bfloat16)
    return high, low


def inner_tables():
    table = cosine64(256)
    swapped = table.reshape(32, 2, 4, 256)[:, ::-1].reshape(256, 256)
    return two(np.stack([table, swapped]))


def split(x):
    high = x.astype(BF16)
    return high, (x - high.astype(F32)).astype(BF16)


def dot(a, b, dims=(((1,), (0,)), ((), ()))):
    return lax.dot_general(a, b, dims, preferred_element_type=F32)


def inner_kernel(start, sign_ref, high_ref, low_ref, x_ref, out_ref):
    results = []
    for s in range(2):
        place = 4 * (start + pl.program_id(0)) + 2 * s
        bits = jnp.concatenate([sign_ref[pl.ds(place, 1), :], sign_ref[pl.ds(place + 1, 1), :]], axis=1)
        sign = (1 - 2 * bits).astype(F32).astype(BF16)
        ch, cl = high_ref[s] * sign, low_ref[s] * sign
        xh, xl = split(x_ref[s * 256 : (s + 1) * 256, :])
        results.append((dot(ch, xh) + (dot(cl, xh) + dot(ch, xl))).reshape(32, 8, 512))
    first, second = results
    upper = lax.broadcasted_iota(jnp.int32, first.shape, 1) < 4
    out_ref[:, 0, 0] = jnp.where(upper, first, second)
    out_ref[:, 1, 0] = jnp.where(upper, second, first)


def inner(matrix, sign_bits, start, count):
    high, low = inner_tables()
    whole = pl.BlockSpec((2, 256, 256), lambda b: (0, 0, 0))
    return pl.pallas_call(
        functools.partial(inner_kernel, start),
        grid=(count,),
        in_specs=[
            pl.BlockSpec((matrix.shape[0] // 128, 128), lambda b: (0, 0)),
            whole,
            whole,
            pl.BlockSpec((512, 512), lambda b: (start + b, 0)),
        ],
        out_specs=pl.BlockSpec((32, 2, 1, 8, 512), lambda b: (0, 0, b, 0, 0)),
        out_shape=jax.ShapeDtypeStruct((32, 2, count, 8, 512), F32),
        cost_estimate=pl.CostEstimate(flops=count * 6 * 512 * 256 * 512, bytes_accessed=count * 2**21, transcendentals=0),
        name="inner",
    )(sign_bits.reshape(-1, 128), jnp.asarray(high), jnp.asarray(low), matrix)


def parity_kernel(first_ref, samples_ref, out_ref):
    batches, half = samples_ref.shape[0], samples_ref.shape[1]
    first = first_ref[0]
    step = 2048
    for b in range(batches):
        total = jnp.zeros((8, 128), F32)
        for start in range(0, half, step):
            pos = samples_ref[b : b + 1, start : start + step]
            a = lax.shift_right_logical(pos, 8)
            pair = lax.shift_right_logical(lax.bitwise_and(pos, 255), 1) - first
            odd = lax.bitwise_and(pos, 1)
            rows = lax.broadcasted_iota(jnp.int32, (128, step), 0)
            hot = (rows == a).astype(F32).astype(BF16)
            which = lax.broadcasted_iota(jnp.int32, (8, step), 0)
            mine = jnp.where(which == pair, odd, 0).astype(F32).astype(BF16)
            total = total + dot(mine, hot, NT)
        out_ref[b] = total


def parity(samples, first_pair):
    batches, half = samples.shape
    return pl.pallas_call(
        parity_kernel,
        grid_spec=pltpu.PrefetchScalarGridSpec(
            num_scalar_prefetch=1,
            grid=(1,),
            in_specs=[pl.BlockSpec((batches, half), lambda i, f: (0, 0))],
            out_specs=pl.BlockSpec((batches, 8, 128), lambda i, f: (0, 0, 0)),
        ),
        out_shape=jax.ShapeDtypeStruct((batches, 8, 128), F32),
        cost_estimate=pl.CostEstimate(flops=2 * batches * half * 128 * 8, bytes_accessed=4 * batches * half, transcendentals=0),
        name="parity",
    )(first_pair, samples)


def outer_kernel(scale, steps, par_ref, odd_ref, high_ref, low_ref, z_ref, prev_ref, *refs):
    step = pl.program_id(0)
    acc_ref, wide_ref = refs[-2:]

    @pl.when(step == 0)
    def _():
        acc_ref[...] = jnp.zeros((512, 512), F32) if prev_ref is None else prev_ref[...]
        place = lax.broadcasted_iota(jnp.int32, (128, 512), 0)
        col = lax.broadcasted_iota(jnp.int32, (128, 512), 1)
        source = 2 * lax.shift_right_logical(col, 3) + lax.bitwise_xor(
            lax.bitwise_and(lax.shift_right_logical(col, 2), 1), par_ref[0]
        )
        pick = jnp.where(place == source, 1.0, 0.0).astype(BF16)
        wide_ref[0] = dot(high_ref[...], pick).astype(BF16)
        wide_ref[1] = dot(low_ref[...], pick).astype(BF16)

    z = z_ref[:, 0].reshape(512, 512)
    zh, zl = split(z)
    row = lax.broadcasted_iota(jnp.int32, (256, 512), 0)
    col = lax.broadcasted_iota(jnp.int32, (256, 512), 1)
    choice = 2 * lax.shift_right_logical(row, 7) + odd_ref[0].astype(jnp.int32)
    keep = jnp.where(lax.bitwise_and(col, 3) == choice, 1.0, 0.0).astype(BF16)
    wh = jnp.concatenate([wide_ref[0]] * 2, axis=0) * keep
    wl = jnp.concatenate([wide_ref[1]] * 2, axis=0) * keep
    rows = dot(wh, zh) + (dot(wl, zh) + dot(wh, zl))
    rh, rl = split(rows)
    acc_ref[...] += dot(rh, rh, TN) + (dot(rh, rl, TN) + dot(rl, rh, TN))

    @pl.when(step == steps - 1)
    def _():
        if scale is None:
            refs[0][...] = acc_ref[...]
        else:
            mine = pl.multiple_of(256 * par_ref[0], 256)
            refs[0][...] = acc_ref[pl.ds(mine, 256), :] * scale
            refs[1][...] = acc_ref[pl.ds(256 - mine, 256), :] * scale


def outer(mixed, odd, start, par, prev, scale):
    count = mixed.shape[1]
    high, low = two(cosine64(128))
    table = pl.BlockSpec((128, 128), lambda b, p: (0, 0))
    whole = pl.BlockSpec((512, 512), lambda b, p: (0, 0))
    half = pl.BlockSpec((256, 512), lambda b, p: (0, 0))
    body = functools.partial(outer_kernel, scale, count)
    if prev is None:
        kernel = lambda p, o, h, l, z, *refs: body(p, o, h, l, z, None, *refs)
    else:
        kernel = body
    return pl.pallas_call(
        kernel,
        grid_spec=pltpu.PrefetchScalarGridSpec(
            num_scalar_prefetch=1,
            grid=(count,),
            in_specs=[
                pl.BlockSpec((1, 256, 1), lambda b, p: (start + b, 0, 0)),
                table,
                table,
                pl.BlockSpec((64, 1, 8, 512), lambda b, p: (0, b, 0, 0)),
            ]
            + ([] if prev is None else [whole]),
            out_specs=whole if scale is None else [half, half],
            scratch_shapes=[pltpu.VMEM((512, 512), F32), pltpu.VMEM((2, 128, 512), BF16)],
        ),
        out_shape=jax.ShapeDtypeStruct((512, 512), F32)
        if scale is None
        else [jax.ShapeDtypeStruct((256, 512), F32)] * 2,
        cost_estimate=pl.CostEstimate(flops=count * 12 * 256 * 512 * 512, bytes_accessed=count * 2**20, transcendentals=0),
        name="outer",
    )(par, odd, jnp.asarray(high), jnp.asarray(low), mixed, *([] if prev is None else [prev]))


def hdot(a, b, dims=(((1,), (0,)), ((), ()))):
    return lax.dot_general(a, b, dims, precision=lax.Precision.HIGHEST, preferred_element_type=F32)


PANEL, GROUP = 32, 16


def thirds(x):
    first = x.astype(BF16)
    rest = x - first.astype(F32)
    second = rest.astype(BF16)
    return first, second, (rest - second.astype(F32)).astype(BF16)


def sixfold(a, b):
    ap, bp = thirds(a), thirds(b)
    order = ((2, 0), (0, 2), (1, 1), (1, 0), (0, 1), (0, 0))
    return dot(
        jnp.concatenate([ap[p] for p, _ in order], axis=0), jnp.concatenate([bp[q] for _, q in order], axis=0), TN
    )


def factor(block):
    size = block.shape[0]
    lane = lax.broadcasted_iota(jnp.int32, (8, size), 1)
    sub = lax.broadcasted_iota(jnp.int32, (8, size), 0)
    rows = [block[8 * i : 8 * i + 8] for i in range(size // 8)]
    pivots = []

    def along(x, c):
        return jnp.broadcast_to(x[:, c : c + 1], (8, size))

    def down(x, j):
        return jnp.broadcast_to(x[j : j + 1, :], (8, size))

    def within(start, stop):
        return (lane >= start) & (lane < stop)

    for base in range(0, size, PANEL):
        end = base + PANEL
        for first in range(base, end, GROUP):
            mine = range(first // 8, (first + GROUP) // 8)
            below = range((first + GROUP) // 8, end // 8)
            inside = within(first, first + GROUP)
            cols = {}
            for k in range(GROUP):
                for i in (*mine, *below):
                    cols[i, k] = along(rows[i], first + k)
            for i in mine:
                rows[i] = jnp.where(inside, jnp.where(lane == sub + 8 * i, 1.0, 0.0), rows[i])
            for i in below:
                rows[i] = jnp.where(inside, 0.0, rows[i])
            for j in range(GROUP):
                at, r = (first + j) // 8, j % 8
                inverse = 1.0 / down(cols[at, j], r)
                heads = {k: down(cols[at, k], r) for k in range(j + 1, GROUP)}
                line = down(rows[at], r)
                for i in range(at, end // 8):
                    if i == at and r == 7:
                        continue
                    multiple = cols[i, j] * inverse
                    if i == at:
                        multiple = jnp.where(sub > r, multiple, 0.0)
                    for k in range(j + 1, GROUP):
                        cols[i, k] = cols[i, k] - multiple * heads[k]
                    rows[i] = rows[i] - multiple * line
            for i in mine:
                pivot = cols[i, 8 * i - first]
                for k in range(GROUP):
                    rows[i] = jnp.where((lane == first + k) & (sub + 8 * i <= first + k), cols[i, k], rows[i])
                    if 0 < first + k - 8 * i < 8:
                        pivot = jnp.where(sub == first + k - 8 * i, cols[i, k], pivot)
                pivots.append(pivot)
        if end < size:
            mine = range(base // 8, end // 8)
            inside = within(base, end)
            left = [jnp.where(lane >= end, rows[i] / pivots[i], 0.0) for i in mine]
            right = []
            for i in mine:
                unit = jnp.where(lane == sub + 8 * i, 1.0, jnp.where(lane > sub + 8 * i, 0.0, rows[i]))
                right.append(jnp.where(inside, unit, rows[i]))
            change = sixfold(jnp.concatenate(left, axis=0), jnp.concatenate(right, axis=0))
            for i in range(end // 8, size // 8):
                rows[i] = jnp.where(inside, 0.0, rows[i]) - change[8 * i : 8 * i + 8]
    return jnp.concatenate(rows, axis=0), jnp.concatenate(pivots, axis=0)


def product(lhs, blocks):
    n = blocks[0].shape[1]
    stack = []
    for block in blocks:
        high, low = split(block)
        stack.append(jnp.concatenate([high, low], axis=1))
        stack.append(jnp.concatenate([high, jnp.zeros_like(low)], axis=1))
    both = dot(lhs, jnp.concatenate(stack, axis=0))
    return both[:, :n] + both[:, n:]


def solve_kernel(par_ref, own_ref, other_ref, x_hbm, r_ref, out_hbm, g_ref, inv_ref, x_ref, xs_ref, out_ref, in_sem, out_sem):
    n, nb = 512, 128
    count = n // nb
    fetch = pltpu.make_async_copy(x_hbm, x_ref, in_sem)
    fetch.start()
    mine = pl.multiple_of(256 * par_ref[0], 256)
    g_ref[pl.ds(mine, 256), :] = own_ref[...]
    g_ref[pl.ds(256 - mine, 256), :] = other_ref[...]
    inv_ref[...] = jnp.zeros((n, n), F32)
    r_ref[...] = jnp.zeros((n, n), F32)
    row = lax.broadcasted_iota(jnp.int32, (nb, nb), 0)
    col = lax.broadcasted_iota(jnp.int32, (nb, nb), 1)
    stores = []
    for k in range(count):
        lo, hi = k * nb, (k + 1) * nb
        if k > 0:
            t = hdot(inv_ref[:lo, :lo], r_ref[:lo, lo:hi])
            base = x_ref[:, lo:hi] - product(xs_ref[:, : 2 * lo], [t[i : i + nb] for i in range(0, lo, nb)])
            lhs = jnp.concatenate(split(base), axis=1)
        m, pivots = factor(g_ref[lo:hi, lo:hi])
        root = lax.rsqrt(pivots)
        root = root * (1.5 - 0.5 * pivots * root * root)
        upper = jnp.where(col >= row, m, 0.0) * root
        linv = jnp.where(col < row, m, jnp.where(col == row, 1.0, 0.0)) * root
        r_ref[lo:hi, lo:hi] = upper
        panels = {}
        for j in range(k + 1, count):
            a, b = j * nb, (j + 1) * nb
            panels[j] = hdot(linv, g_ref[lo:hi, a:b])
            r_ref[lo:hi, a:b] = panels[j]
            for i in range(k + 1, j + 1):
                c, d = i * nb, (i + 1) * nb
                g_ref[c:d, a:b] -= hdot(panels[i], panels[j], TN)
        rinv = linv.T
        if k + 1 < count:
            inv_ref[lo:hi, lo:hi] = rinv
            if k > 0:
                inv_ref[:lo, lo:hi] = -hdot(t, rinv)
        if k == 0:
            fetch.wait()
            for i in range(count):
                xs_ref[:, 2 * i * nb : 2 * (i + 1) * nb] = jnp.concatenate(split(x_ref[:, i * nb : (i + 1) * nb]), axis=1)
            lhs = xs_ref[:, : 2 * nb]
        out_ref[k] = product(lhs, [rinv])
        store = pltpu.make_async_copy(out_ref.at[k], out_hbm.at[:, lo:hi], out_sem.at[k])
        store.start()
        stores.append(store)
    for store in stores:
        store.wait()


def solve(par, own, other, matrix):
    rows, n = matrix.shape
    vmem = pl.BlockSpec(memory_space=pltpu.VMEM)
    smem = pl.BlockSpec(memory_space=pltpu.SMEM)
    hbm = pl.BlockSpec(memory_space=pltpu.HBM)
    return pl.pallas_call(
        solve_kernel,
        in_specs=[smem, vmem, vmem, hbm],
        out_specs=(vmem, hbm),
        out_shape=(jax.ShapeDtypeStruct((n, n), F32), jax.ShapeDtypeStruct((rows, n), F32)),
        scratch_shapes=[
            pltpu.VMEM((n, n), F32),
            pltpu.VMEM((n, n), F32),
            pltpu.VMEM((rows, n), F32),
            pltpu.VMEM((rows, 2 * n), BF16),
            pltpu.VMEM((n // 128, rows, 128), F32),
            pltpu.SemaphoreType.DMA,
            pltpu.SemaphoreType.DMA((n // 128,)),
        ],
        compiler_params=pltpu.CompilerParams(vmem_limit_bytes=61 * 2**20),
        name="solve",
    )(par, own, other, matrix)


def exchange(x, axes):
    return lax.all_to_all(x, axes, split_axis=0, concat_axis=0, tiled=True)


def spread(x, copies, axes):
    return exchange(jnp.broadcast_to(x[None], (copies,) + x.shape), axes)


def local(matrix, sign_bits, samples):
    batches, half = samples.shape
    core = lax.axis_index("core").astype(jnp.int32)
    device = lax.axis_index(("z", "y", "core")).astype(jnp.int32)
    par = core.reshape(1)
    mixed = []
    start = 0
    for count in (batches,):
        sent = inner(matrix, sign_bits, start, count).reshape(64, count, 8, 512)
        mixed.append(exchange(sent, ("z", "y", "core")))
        start += count
    odd = parity(samples, (2 * device).reshape(1))[:, :2].reshape(batches, 256, 1)
    start, total = 0, None
    for i, count in enumerate((batches,)):
        last = i == len(mixed) - 1
        total = outer(mixed[i], odd, start, par, total, 1.0 / (4 * batches * half) if last else None)
        start += count
    keep, send = total
    swap = [(0, 1), (1, 0)]
    part = keep + lax.ppermute(send, "core", swap)
    part = exchange(part.reshape(16, 16, 512), ("y", "x")).sum(0)
    part = spread(part, 8, "z").sum(0)
    own = spread(part, 16, ("y", "x")).reshape(256, 512)
    other = lax.ppermute(own, "core", swap)
    return solve(par, own, other, matrix)


def solution(mesh):
    parts = Mesh(mesh.devices.reshape(8, 4, 2, 4), ("z", "y", "core", "x"))
    every = ("z", "y", "core", "x")
    return jax.shard_map(
        local,
        mesh=parts,
        in_specs=(P(every, None), P(every), P("x", None)),
        out_specs=(P(), P(every, None)),
        check_vma=False,
    )
```

```python
import functools
import numpy as np
import jax
import jax.numpy as jnp
from jax import lax
from jax.sharding import Mesh
from jax.sharding import PartitionSpec as P
from jax.experimental import pallas as pl
from jax.experimental.pallas import tpu as pltpu

F32, BF16 = jnp.float32, jnp.bfloat16
INNER_STEP, OUTER_STEP = 2, 2
NT = (((1,), (1,)), ((), ()))
TN = (((0,), (0,)), ((), ()))


def cosine64(size):
    freq = np.arange(size)[:, None]
    place = np.arange(size)[None, :]
    weight = np.where(freq == 0, 1.0, 2.0) / size
    return np.sqrt(weight) * np.cos(np.pi * ((2 * place + 1) * freq % (4 * size)) / (2 * size))


def two(table):
    high = table.astype(np.float32).astype(jnp.bfloat16)
    low = (table - high.astype(np.float64)).astype(np.float32).astype(jnp.bfloat16)
    return high, low


def inner_tables():
    table = cosine64(256)
    swapped = table.reshape(32, 2, 4, 256)[:, ::-1].reshape(256, 256)
    return two(np.stack([table, swapped]))


def split(x):
    high = x.astype(BF16)
    return high, (x - high.astype(F32)).astype(BF16)


def dot(a, b, dims=(((1,), (0,)), ((), ()))):
    return lax.dot_general(a, b, dims, preferred_element_type=F32)


def inner_kernel(sign_ref, high_ref, low_ref, x_ref, out_ref):
    per = out_ref.shape[2]
    for u in range(per):
        results = []
        for s in range(2):
            place = 4 * (per * pl.program_id(0) + u) + 2 * s
            bits = jnp.concatenate([sign_ref[pl.ds(place, 1), :], sign_ref[pl.ds(place + 1, 1), :]], axis=1)
            sign = (1 - 2 * bits).astype(F32).astype(BF16)
            ch, cl = high_ref[s] * sign, low_ref[s] * sign
            xh, xl = split(x_ref[512 * u + 256 * s : 512 * u + 256 * (s + 1), :])
            results.append((dot(ch, xh) + (dot(cl, xh) + dot(ch, xl))).reshape(32, 8, 512))
        first, second = results
        upper = lax.broadcasted_iota(jnp.int32, first.shape, 1) < 4
        out_ref[:, 0, u] = jnp.where(upper, first, second)
        out_ref[:, 1, u] = jnp.where(upper, second, first)


def inner(matrix, sign_bits, per):
    count = matrix.shape[0] // 512
    high, low = inner_tables()
    whole = pl.BlockSpec((2, 256, 256), lambda b: (0, 0, 0))
    return pl.pallas_call(
        inner_kernel,
        grid=(count // per,),
        in_specs=[
            pl.BlockSpec((4 * count, 128), lambda b: (0, 0)),
            whole,
            whole,
            pl.BlockSpec((512 * per, 512), lambda b: (b, 0)),
        ],
        out_specs=pl.BlockSpec((32, 2, per, 8, 512), lambda b: (0, 0, b, 0, 0)),
        out_shape=jax.ShapeDtypeStruct((32, 2, count, 8, 512), F32),
        cost_estimate=pl.CostEstimate(flops=count * 6 * 512 * 256 * 512, bytes_accessed=count * 2**21, transcendentals=0),
        name="inner",
    )(sign_bits.reshape(-1, 128), jnp.asarray(high), jnp.asarray(low), matrix)


def parity_kernel(first_ref, samples_ref, out_ref):
    batches, half = samples_ref.shape[0], samples_ref.shape[1]
    first = first_ref[0]
    step = 2048
    for b in range(batches):
        total = jnp.zeros((8, 128), F32)
        for start in range(0, half, step):
            pos = samples_ref[b : b + 1, start : start + step]
            a = lax.shift_right_logical(pos, 8)
            pair = lax.shift_right_logical(lax.bitwise_and(pos, 255), 1) - first
            odd = lax.bitwise_and(pos, 1)
            rows = lax.broadcasted_iota(jnp.int32, (128, step), 0)
            hot = (rows == a).astype(F32).astype(BF16)
            which = lax.broadcasted_iota(jnp.int32, (8, step), 0)
            mine = jnp.where(which == pair, odd, 0).astype(F32).astype(BF16)
            total = total + dot(mine, hot, NT)
        out_ref[b] = total


def parity(samples, first_pair):
    batches, half = samples.shape
    return pl.pallas_call(
        parity_kernel,
        grid_spec=pltpu.PrefetchScalarGridSpec(
            num_scalar_prefetch=1,
            grid=(1,),
            in_specs=[pl.BlockSpec((batches, half), lambda i, f: (0, 0))],
            out_specs=pl.BlockSpec((batches, 8, 128), lambda i, f: (0, 0, 0)),
        ),
        out_shape=jax.ShapeDtypeStruct((batches, 8, 128), F32),
        cost_estimate=pl.CostEstimate(flops=2 * batches * half * 128 * 8, bytes_accessed=4 * batches * half, transcendentals=0),
        name="parity",
    )(first_pair, samples)


def outer_kernel(scale, steps, par_ref, odd_ref, high_ref, low_ref, z_ref, keep_ref, send_ref, acc_ref, wide_ref):
    step = pl.program_id(0)

    @pl.when(step == 0)
    def _():
        acc_ref[...] = jnp.zeros((512, 512), F32)
        place = lax.broadcasted_iota(jnp.int32, (128, 512), 0)
        col = lax.broadcasted_iota(jnp.int32, (128, 512), 1)
        source = 2 * lax.shift_right_logical(col, 3) + lax.bitwise_xor(
            lax.bitwise_and(lax.shift_right_logical(col, 2), 1), par_ref[0]
        )
        pick = jnp.where(place == source, 1.0, 0.0).astype(BF16)
        wide_ref[0] = dot(high_ref[...], pick).astype(BF16)
        wide_ref[1] = dot(low_ref[...], pick).astype(BF16)

    total = None
    for u in range(z_ref.shape[1]):
        zh, zl = split(z_ref[:, u].reshape(512, 512))
        row = lax.broadcasted_iota(jnp.int32, (256, 512), 0)
        col = lax.broadcasted_iota(jnp.int32, (256, 512), 1)
        choice = 2 * lax.shift_right_logical(row, 7) + odd_ref[u].astype(jnp.int32)
        keep = jnp.where(lax.bitwise_and(col, 3) == choice, 1.0, 0.0).astype(BF16)
        wh = jnp.concatenate([wide_ref[0]] * 2, axis=0) * keep
        wl = jnp.concatenate([wide_ref[1]] * 2, axis=0) * keep
        rows = dot(wh, zh) + (dot(wl, zh) + dot(wh, zl))
        rh, rl = split(rows)
        part = dot(rh, rh, TN) + (dot(rh, rl, TN) + dot(rl, rh, TN))
        total = part if total is None else total + part
    acc_ref[...] += total

    @pl.when(step == steps - 1)
    def _():
        mine = pl.multiple_of(256 * par_ref[0], 256)
        keep_ref[...] = acc_ref[pl.ds(mine, 256), :] * scale
        send_ref[...] = acc_ref[pl.ds(256 - mine, 256), :] * scale


def outer(mixed, odd, par, scale, per):
    count = mixed.shape[1]
    high, low = two(cosine64(128))
    table = pl.BlockSpec((128, 128), lambda b, p: (0, 0))
    half = pl.BlockSpec((256, 512), lambda b, p: (0, 0))
    return pl.pallas_call(
        functools.partial(outer_kernel, scale, count // per),
        grid_spec=pltpu.PrefetchScalarGridSpec(
            num_scalar_prefetch=1,
            grid=(count // per,),
            in_specs=[
                pl.BlockSpec((per, 256, 1), lambda b, p: (b, 0, 0)),
                table,
                table,
                pl.BlockSpec((64, per, 8, 512), lambda b, p: (0, b, 0, 0)),
            ],
            out_specs=[half, half],
            scratch_shapes=[pltpu.VMEM((512, 512), F32), pltpu.VMEM((2, 128, 512), BF16)],
        ),
        out_shape=[jax.ShapeDtypeStruct((256, 512), F32)] * 2,
        cost_estimate=pl.CostEstimate(flops=count * 12 * 256 * 512 * 512, bytes_accessed=count * 2**20, transcendentals=0),
        name="outer",
    )(par, odd, jnp.asarray(high), jnp.asarray(low), mixed)


def hdot(a, b, dims=(((1,), (0,)), ((), ()))):
    return lax.dot_general(a, b, dims, precision=lax.Precision.HIGHEST, preferred_element_type=F32)


PANEL, GROUP = 32, 16


def thirds(x):
    first = x.astype(BF16)
    rest = x - first.astype(F32)
    second = rest.astype(BF16)
    return first, second, (rest - second.astype(F32)).astype(BF16)


def sixfold(a, b):
    ap, bp = thirds(a), thirds(b)
    order = ((2, 0), (0, 2), (1, 1), (1, 0), (0, 1), (0, 0))
    return dot(
        jnp.concatenate([ap[p] for p, _ in order], axis=0), jnp.concatenate([bp[q] for _, q in order], axis=0), TN
    )


def factor(block):
    size = block.shape[0]
    lane = lax.broadcasted_iota(jnp.int32, (8, size), 1)
    sub = lax.broadcasted_iota(jnp.int32, (8, size), 0)
    rows = [block[8 * i : 8 * i + 8] for i in range(size // 8)]
    pivots = []

    def along(x, c):
        return jnp.broadcast_to(x[:, c : c + 1], (8, size))

    def down(x, j):
        return jnp.broadcast_to(x[j : j + 1, :], (8, size))

    def within(start, stop):
        return (lane >= start) & (lane < stop)

    for base in range(0, size, PANEL):
        end = base + PANEL
        for first in range(base, end, GROUP):
            mine = range(first // 8, (first + GROUP) // 8)
            below = range((first + GROUP) // 8, end // 8)
            inside = within(first, first + GROUP)
            cols = {}
            for k in range(GROUP):
                for i in (*mine, *below):
                    cols[i, k] = along(rows[i], first + k) + 0.0
            for i in mine:
                rows[i] = jnp.where(inside, jnp.where(lane == sub + 8 * i, 1.0, 0.0), rows[i])
            for i in below:
                rows[i] = jnp.where(inside, 0.0, rows[i])
            for j in range(GROUP):
                at, r = (first + j) // 8, j % 8
                inverse = 1.0 / down(cols[at, j], r)
                heads = {k: down(cols[at, k], r) for k in range(j + 1, GROUP)}
                line = down(rows[at], r)
                for i in range(at, end // 8):
                    if i == at and r == 7:
                        continue
                    multiple = cols[i, j] * inverse
                    if i == at:
                        multiple = jnp.where(sub > r, multiple, 0.0)
                    for k in range(j + 1, GROUP):
                        cols[i, k] = cols[i, k] - multiple * heads[k]
                    rows[i] = rows[i] - multiple * line
            for i in mine:
                pivot = cols[i, 8 * i - first]
                for k in range(GROUP):
                    rows[i] = jnp.where((lane == first + k) & (sub + 8 * i <= first + k), cols[i, k], rows[i])
                    if 0 < first + k - 8 * i < 8:
                        pivot = jnp.where(sub == first + k - 8 * i, cols[i, k], pivot)
                pivots.append(pivot)
        if end < size:
            mine = range(base // 8, end // 8)
            inside = within(base, end)
            left = [jnp.where(lane >= end, rows[i] / pivots[i], 0.0) for i in mine]
            right = []
            for i in mine:
                unit = jnp.where(lane == sub + 8 * i, 1.0, jnp.where(lane > sub + 8 * i, 0.0, rows[i]))
                right.append(jnp.where(inside, unit, rows[i]))
            change = sixfold(jnp.concatenate(left, axis=0), jnp.concatenate(right, axis=0))
            for i in range(end // 8, size // 8):
                rows[i] = jnp.where(inside, 0.0, rows[i]) - change[8 * i : 8 * i + 8]
    return jnp.concatenate(rows, axis=0), jnp.concatenate(pivots, axis=0)


def product(lhs, blocks):
    n = blocks[0].shape[1]
    stack = []
    for block in blocks:
        high, low = split(block)
        stack.append(jnp.concatenate([high, low], axis=1))
        stack.append(jnp.concatenate([high, jnp.zeros_like(low)], axis=1))
    both = dot(lhs, jnp.concatenate(stack, axis=0))
    return both[:, :n] + both[:, n:]


def solve_kernel(par_ref, own_ref, other_ref, x_hbm, r_ref, out_hbm, g_ref, inv_ref, x_ref, xs_ref, out_ref, in_sem, out_sem):
    n, nb = 512, 128
    count = n // nb
    fetch = pltpu.make_async_copy(x_hbm, x_ref, in_sem)
    fetch.start()
    mine = pl.multiple_of(256 * par_ref[0], 256)
    g_ref[pl.ds(mine, 256), :] = own_ref[...]
    g_ref[pl.ds(256 - mine, 256), :] = other_ref[...]
    inv_ref[...] = jnp.zeros((n, n), F32)
    r_ref[...] = jnp.zeros((n, n), F32)
    row = lax.broadcasted_iota(jnp.int32, (nb, nb), 0)
    col = lax.broadcasted_iota(jnp.int32, (nb, nb), 1)
    stores = []
    for k in range(count):
        lo, hi = k * nb, (k + 1) * nb
        if k > 0:
            t = hdot(inv_ref[:lo, :lo], r_ref[:lo, lo:hi])
            base = x_ref[:, lo:hi] - product(xs_ref[:, : 2 * lo], [t[i : i + nb] for i in range(0, lo, nb)])
            lhs = jnp.concatenate(split(base), axis=1)
        m, pivots = factor(g_ref[lo:hi, lo:hi])
        root = lax.rsqrt(pivots)
        root = root * (1.5 - 0.5 * pivots * root * root)
        upper = jnp.where(col >= row, m, 0.0) * root
        linv = jnp.where(col < row, m, jnp.where(col == row, 1.0, 0.0)) * root
        r_ref[lo:hi, lo:hi] = upper
        panels = {}
        for j in range(k + 1, count):
            a, b = j * nb, (j + 1) * nb
            panels[j] = hdot(linv, g_ref[lo:hi, a:b])
            r_ref[lo:hi, a:b] = panels[j]
            for i in range(k + 1, j + 1):
                c, d = i * nb, (i + 1) * nb
                g_ref[c:d, a:b] -= hdot(panels[i], panels[j], TN)
        rinv = linv.T
        if k + 1 < count:
            inv_ref[lo:hi, lo:hi] = rinv
            if k > 0:
                inv_ref[:lo, lo:hi] = -hdot(t, rinv)
        if k == 0:
            fetch.wait()
            for i in range(count):
                xs_ref[:, 2 * i * nb : 2 * (i + 1) * nb] = jnp.concatenate(split(x_ref[:, i * nb : (i + 1) * nb]), axis=1)
            lhs = xs_ref[:, : 2 * nb]
        out_ref[k] = product(lhs, [rinv])
        store = pltpu.make_async_copy(out_ref.at[k], out_hbm.at[:, lo:hi], out_sem.at[k])
        store.start()
        stores.append(store)
    for store in stores:
        store.wait()


def solve(par, own, other, matrix):
    rows, n = matrix.shape
    vmem = pl.BlockSpec(memory_space=pltpu.VMEM)
    smem = pl.BlockSpec(memory_space=pltpu.SMEM)
    hbm = pl.BlockSpec(memory_space=pltpu.HBM)
    return pl.pallas_call(
        solve_kernel,
        in_specs=[smem, vmem, vmem, hbm],
        out_specs=(vmem, hbm),
        out_shape=(jax.ShapeDtypeStruct((n, n), F32), jax.ShapeDtypeStruct((rows, n), F32)),
        scratch_shapes=[
            pltpu.VMEM((n, n), F32),
            pltpu.VMEM((n, n), F32),
            pltpu.VMEM((rows, n), F32),
            pltpu.VMEM((rows, 2 * n), BF16),
            pltpu.VMEM((n // 128, rows, 128), F32),
            pltpu.SemaphoreType.DMA,
            pltpu.SemaphoreType.DMA((n // 128,)),
        ],
        compiler_params=pltpu.CompilerParams(vmem_limit_bytes=61 * 2**20),
        name="solve",
    )(par, own, other, matrix)


def exchange(x, axes):
    return lax.all_to_all(x, axes, split_axis=0, concat_axis=0, tiled=True)


def spread(x, copies, axes):
    return exchange(jnp.broadcast_to(x[None], (copies,) + x.shape), axes)


def local(matrix, sign_bits, samples):
    batches, half = samples.shape
    core = lax.axis_index("core").astype(jnp.int32)
    device = lax.axis_index(("z", "y", "core")).astype(jnp.int32)
    par = core.reshape(1)
    sent = inner(matrix, sign_bits, INNER_STEP).reshape(64, batches, 8, 512)
    mixed = exchange(sent, ("z", "y", "core"))
    odd = parity(samples, (2 * device).reshape(1))[:, :2].reshape(batches, 256, 1)
    keep, send = outer(mixed, odd, par, 1.0 / (4 * batches * half), OUTER_STEP)
    swap = [(0, 1), (1, 0)]
    part = keep + lax.ppermute(send, "core", swap)
    part = exchange(part.reshape(16, 16, 512), ("y", "x")).sum(0)
    part = spread(part, 8, "z").sum(0)
    own = spread(part, 16, ("y", "x")).reshape(256, 512)
    other = lax.ppermute(own, "core", swap)
    return solve(par, own, other, matrix)


def solution(mesh):
    parts = Mesh(mesh.devices.reshape(8, 4, 2, 4), ("z", "y", "core", "x"))
    every = ("z", "y", "core", "x")
    return jax.shard_map(
        local,
        mesh=parts,
        in_specs=(P(every, None), P(every), P("x", None)),
        out_specs=(P(), P(every, None)),
        check_vma=False,
    )
```
